128 devices in a mesh: dom: 16 (over x, y), grp: 8 (over z, core).
Axes of the slice: x: 4, y: 4, z: 4, core: 2. Of those that a mesh axis runs over, the one named last changes fastest.
Arguments:
- solved: bfloat16 [16, 8192, 512], P('dom', 'grp'), may hold values from -6 to 6
- e_blocks: bfloat16 [16, 6, 8192, 1024], P('dom', None, 'grp'), may hold values from -0.09375 to 0.09375
- block_mask: int32 [16, 6, 8], P('dom', None, 'grp'), may hold values 0 or 1
- owner: int32 [16, 6, 1], P('dom'), may hold values from 0 to 15; in each aligned block of 6 rows (0 to 5, 6 to 11, ..., all dimensions but the last counted through in order) at most 2 rows name the same one
- local_id: int32 [16, 6], P('dom'), may hold values from 0 to 3
Outputs:
- schur: bfloat16 [64, 1024, 512], P('dom', 'grp')
The draws below stay inside these ranges and needn't reach their ends.
Inputs may be any that keep to these rules, and one draw needn't show every extreme that they name: Among the 6 slots of one subdomain at most 2 have the same owner, and in some subdomain exactly 2 do.
All inputs are finite; a program needn't handle non-finite values. No bound on the sum of `block_mask` on one device may be relied on, other than what follows from the above.
Results may differ from the reference program's by a relative error of at most 0.015.
Values may be sent and summed in bfloat16 or wider, within the bound.
No kernel may reach another device: no remote copies, remote signals or barrier semaphores. Data moves between devices by JAX's collectives and lax.ppermute only.
A program may use at most 128 MiB of HBM per device.

```python
import math
import jax
import jax.numpy as jnp
import numpy as np
from jax import lax

BLK = 1024
COLS = 512
SLOTS = 6
RBLK_DEV = 1
OWN = 4
CAP = 2
NRB = 8
ROWS = 8192
N_DOM = 16
N_GRP = 8


def place_ends(result, key, least, high):
    longest = result.shape.index(max(result.shape))
    spots = []
    for shift in (0, 1):
        where = [jax.random.randint(jax.random.fold_in(key, axis), (), 0, length) for axis, length in enumerate(result.shape)]
        where[longest] = (where[longest] + shift) % result.shape[longest]
        spots.append(tuple(where))
    return result.at[spots[0]].set(least).at[spots[1]].set(high)


def strengthened(values, stream_key, source, target, shards_of, factor):
    def block_of(dim):
        return (jnp.arange(values.shape[dim]) // (values.shape[dim] // shards_of)).reshape((-1,) + (1,) * (values.ndim - 1 - dim))

    first = jax.random.permutation(stream_key, shards_of)[block_of(target)]
    far = (block_of(target) + shards_of // 2) % shards_of
    return jnp.where((block_of(source) == first) | (block_of(source) == far), factor * values, values)


def block_scale(rng, shape, split, low, top_value):
    factor_of = 1.0
    for axis_at, shards_of in split:
        heights = jax.random.uniform(jax.random.fold_in(jax.random.fold_in(rng, 6), axis_at), (shards_of,), jnp.float32, low / len(split), top_value / len(split))
        factor_of = factor_of * jnp.repeat(jnp.exp(heights), shape[axis_at] // shards_of).reshape((-1,) + (1,) * (len(shape) - 1 - axis_at))
    return factor_of


def routed_block(key, own, number, rows, amount, top, bound, slope):
    ranking = jax.random.permutation(key, amount)
    heavy_load, ordinary = portions_of(amount, rows * top, bound, slope, True), portions_of(amount, rows * top, bound, slope, False)
    places = jnp.arange(amount)

    def named(sizes, turn):
        used = int((sizes > 0).sum())
        fixed = max(1, used // 4)
        shifted = fixed + (places - fixed + turn * (used - fixed)) % max(1, amount - fixed)
        return jnp.zeros((amount,), jnp.int32).at[ranking[jnp.where(places < fixed, places, shifted)]].set(jnp.asarray(sizes, jnp.int32))

    sizes = jnp.where(number % 4 == 0, named(heavy_load, number // 4), named(ordinary, number - number // 4 - 1))
    mixed = jax.random.permutation(jax.random.fold_in(own, 3), amount)
    source_of, sink = mixed[0:amount // 2 * 2:2], mixed[1:amount // 2 * 2:2]
    margin = jnp.minimum(sizes[source_of] - 1, bound - sizes[sink]) // 2
    margin = jnp.where((source_of == ranking[0]) | (sink == ranking[0]) | (sizes[sink] == 0), 0, jnp.maximum(margin, 0))
    shifted = jax.random.randint(jax.random.fold_in(own, 4), (amount // 2,), 0, 1 << 20) % (margin + 1)
    sizes = sizes.at[source_of].add(-shifted).at[sink].add(shifted)
    labels = jnp.searchsorted(jnp.cumsum(sizes), jnp.arange(rows * top), side="right").astype(jnp.int32)
    table = labels.reshape(top, rows).T
    table = table[jax.random.permutation(jax.random.fold_in(own, 1), rows)]
    turn = jax.random.randint(jax.random.fold_in(own, 2), (rows, 1), 0, top)
    return jnp.take_along_axis(table, (jnp.arange(top)[None, :] + turn) % top, axis=1)


def portions_of(count, total, limit, lean, full):
    weights = [(1 << 20) // math.isqrt(rank ** lean) + 1 for rank in range(1, count + 1)]
    largest = limit if full else min(limit, max(-(-total // count), total * weights[0] // sum(weights)))
    least = 1 if total - largest >= count - 1 else 0
    holding, spare = [largest] + [least] * (count - 1), total - largest - least * (count - 1)
    while spare > 0:
        free = [i for i in range(1, count) if holding[i] < largest] or [i for i in range(1, count) if holding[i] < limit]
        mass, left = sum([weights[i] for i in free]), spare
        for i in free:
            extra = min(limit - holding[i], max(1, left * weights[i] // mass), spare)
            holding[i] = holding[i] + extra
            spare = spare - extra
    return np.array(holding)


def noise(own_key, shape, scale, limit, cuts=(), kind=jnp.bfloat16):
    result = scale * jax.random.normal(own_key, shape, jnp.float32)
    if cuts:
        result = result * block_scale(own_key, shape, cuts, -0.22, 0.18)
    return jnp.clip(result, -limit, limit).astype(kind)


def noise_with(stream_key, extent, width, most, cuts, heavy, kind=jnp.bfloat16):
    entries = width * jax.random.normal(stream_key, extent, jnp.float32)
    if cuts:
        entries = entries * block_scale(stream_key, extent, cuts, -0.22, 0.18)
    return jnp.clip(strengthened(entries, jax.random.fold_in(stream_key, 3), *heavy), -most, most).astype(kind)


def setup_inputs(seed: int = 0) -> dict:
    keys = jax.random.split(jax.random.key(seed), 6)
    solved = noise(keys[0], (N_DOM, ROWS, COLS), 1.0, 6.0, ((0, 16), (1, 8)))
    e_blocks = noise_with(keys[1], (N_DOM, SLOTS, ROWS, BLK), ROWS ** -0.5, 0.09375, ((0, 16), (2, 8)), (2, 3, 8, 2.0))
    block_mask = place_ends((jax.random.randint(keys[2], (N_DOM, SLOTS, NRB), 0, 4) < 3).astype(jnp.int32), jax.random.fold_in(keys[2], 1), 0, 1)
    owner_keys = jax.random.split(jax.random.fold_in(keys[3], 1), N_DOM * SLOTS // SLOTS)
    owner_turns = jax.random.permutation(jax.random.fold_in(keys[3], 3), N_DOM * SLOTS // SLOTS)
    owner = jax.vmap(lambda own, number: routed_block(jax.random.fold_in(keys[3], 2), own, number, SLOTS, N_DOM, 1, CAP, 2))(owner_keys, owner_turns).reshape((N_DOM, SLOTS, 1))
    local_id = place_ends(jax.random.randint(keys[4], (N_DOM, SLOTS), 0, OWN), jax.random.fold_in(keys[4], 1), 0, OWN - 1).astype(jnp.int32)
    return {"solved": solved, "e_blocks": e_blocks, "block_mask": block_mask, "owner": owner, "local_id": local_id}


def one_domain(inputs):
    solved_part, coupling, present = inputs
    solved4 = solved_part.reshape(NRB, BLK, COLS).astype(jnp.float32)

    def one_slot(pair):
        slot_coupling, slot_present = pair
        coupling4 = slot_coupling.reshape(NRB, BLK, BLK).astype(jnp.float32)
        product = jnp.einsum("bjk,bjc->bkc", coupling4, solved4)
        weighted = product * slot_present.astype(jnp.float32)[:, None, None]
        partial_value = jnp.sum(weighted.reshape(N_GRP, RBLK_DEV, BLK, COLS), axis=1).astype(jnp.bfloat16)
        return jnp.sum(partial_value.astype(jnp.float32), axis=0).astype(jnp.bfloat16)

    return lax.map(one_slot, (coupling, present))


def reference(solved, e_blocks, block_mask, owner, local_id):
    contribution = lax.map(one_domain, (solved, e_blocks, block_mask))
    target = (owner[:, :, 0] * OWN + local_id).reshape(N_DOM * SLOTS).astype(jnp.int32)
    slots_all = jnp.arange(N_DOM * OWN, dtype=jnp.int32)
    select = (target[:, None] == slots_all[None, :]).astype(jnp.float32)
    flat = contribution.reshape(N_DOM * SLOTS, BLK, COLS).astype(jnp.float32)
    summed = jnp.einsum("nt,nkc->tkc", select, flat)
    return summed.astype(jnp.bfloat16)
```

```python
import functools
import jax
import jax.numpy as jnp
from jax import lax
from jax.experimental import pallas as pl
from jax.experimental.pallas import tpu as pltpu
from jax.sharding import PartitionSpec as P

BLK = 1024
COLS = 512
SLOTS = 6
OWN = 4
N_DOM = 16
N_GRP = 8
N_Z = 4
LANES = BLK // N_GRP
PIECE = COLS // N_DOM
CHUNKS = ((0, 3), (3, 3))


def product_kernel(first, mask_ref, factor_ref, coupling_ref, own0, own1, own2, own3, other, turned):
    group = lax.axis_index("grp")
    plane = lax.div(group, 2)
    core = lax.rem(group, 2)
    slot = pl.program_id(0)

    @pl.when(slot == 0)
    def _():
        turned[...] = factor_ref[0].T

    present = mask_ref[first + slot].astype(jnp.float32)
    for k, own in enumerate((own0, own1, own2, own3)):
        start = pl.multiple_of(lax.rem(plane + k, N_Z) * (2 * LANES), 2 * LANES)
        both = jnp.dot(
            turned[...],
            coupling_ref[:, pl.ds(start, 2 * LANES)],
            preferred_element_type=jnp.float32,
        )
        both = both * present
        low, high = both[:, :LANES], both[:, LANES:]
        mine = jnp.where(core == 0, low, high).astype(jnp.bfloat16)
        theirs = jnp.where(core == 0, high, low).astype(jnp.bfloat16)
        own[...] = mine.reshape(N_DOM, PIECE, LANES)
        other[k] = theirs.reshape(N_DOM, PIECE, LANES)


def product(solved, e_blocks, mask, first, count):
    shape = (N_DOM, count, PIECE, LANES)
    block = (N_DOM, None, PIECE, LANES)
    return pl.pallas_call(
        functools.partial(product_kernel, first),
        grid=(count,),
        in_specs=[
            pl.BlockSpec(memory_space=pltpu.SMEM),
            pl.BlockSpec((1, BLK, COLS), lambda s: (0, 0, 0)),
            pl.BlockSpec((None, None, BLK, BLK), lambda s: (0, first + s, 0, 0)),
        ],
        out_specs=[pl.BlockSpec(block, lambda s: (0, s, 0, 0))] * N_Z
        + [pl.BlockSpec((N_Z,) + block, lambda s: (0, 0, s, 0, 0))],
        out_shape=[jax.ShapeDtypeStruct(shape, jnp.bfloat16)] * N_Z
        + [jax.ShapeDtypeStruct((N_Z,) + shape, jnp.bfloat16)],
        scratch_shapes=[pltpu.VMEM((COLS, BLK), jnp.bfloat16)],
        compiler_params=pltpu.CompilerParams(vmem_limit_bytes=40 << 20),
        name="product",
    )(mask, solved, e_blocks)


def gather_kernel(target_ref, items_ref, out_ref, total):
    total[...] = jnp.zeros_like(total)

    def add(i, _):
        for s in range(SLOTS):
            t = target_ref[i * SLOTS + s]
            total[t] = total[t] + items_ref[i, s].astype(jnp.float32)
        return 0

    lax.fori_loop(0, N_DOM, add, 0)
    out_ref[...] = total[...].astype(jnp.bfloat16)


def sum_blocks(target, items):
    return pl.pallas_call(
        gather_kernel,
        in_specs=[
            pl.BlockSpec(memory_space=pltpu.SMEM),
            pl.BlockSpec(memory_space=pltpu.VMEM),
        ],
        out_specs=pl.BlockSpec(memory_space=pltpu.VMEM),
        out_shape=jax.ShapeDtypeStruct((N_DOM * OWN, PIECE, LANES), jnp.bfloat16),
        scratch_shapes=[pltpu.VMEM((N_DOM * OWN, PIECE, LANES), jnp.float32)],
        compiler_params=pltpu.CompilerParams(vmem_limit_bytes=40 << 20),
        name="sum_blocks",
    )(target, items)


def turn_kernel(pieces_ref, out_ref):
    for l in range(OWN):
        out_ref[l] = pieces_ref[:, l].reshape(COLS, LANES).T


def turn_back(pieces):
    return pl.pallas_call(
        turn_kernel,
        in_specs=[pl.BlockSpec(memory_space=pltpu.VMEM)],
        out_specs=pl.BlockSpec(memory_space=pltpu.VMEM),
        out_shape=jax.ShapeDtypeStruct((OWN, LANES, COLS), jnp.bfloat16),
        compiler_params=pltpu.CompilerParams(vmem_limit_bytes=40 << 20),
        name="turn_back",
    )(pieces)


def total_of(*terms):
    acc = terms[0].astype(jnp.float32)
    for term in terms[1:]:
        acc = acc + term.astype(jnp.float32)
    return acc.astype(jnp.bfloat16)


def shift_z(k):
    return [(g, ((g // 2 + k) % N_Z) * 2 + g % 2) for g in range(N_GRP)]


def on_device(solved, e_blocks, block_mask, owner, local_id):
    mask = block_mask.reshape(SLOTS)
    labels = owner[0, :, 0] * OWN + local_id[0]
    sibling = [(g, g ^ 1) for g in range(N_GRP)]
    half = N_DOM // 2
    reduced = []
    for first, count in CHUNKS:
        own0, own1, own2, own3, other = product(solved, e_blocks, mask, first, count)
        twin = lax.ppermute(other, "grp", sibling)
        far_up = total_of(own2[:half], twin[2, :half])
        far_down = total_of(own2[half:], twin[2, half:])
        from_below = lax.ppermute(far_up, "grp", shift_z(1))
        from_above = lax.ppermute(far_down, "grp", shift_z(-1))
        up = jnp.concatenate(
            [total_of(own1[:half], twin[1, :half], from_below), total_of(own1[half:], twin[1, half:])]
        )
        down = jnp.concatenate(
            [total_of(own3[:half], twin[3, :half]), total_of(own3[half:], twin[3, half:], from_above)]
        )
        low = lax.ppermute(up, "grp", shift_z(1))
        high = lax.ppermute(down, "grp", shift_z(-1))
        reduced.append(total_of(own0, twin[0], low, high))
    everyone = jnp.broadcast_to(labels[None, :], (N_DOM, SLOTS))
    target = lax.all_to_all(everyone, "dom", split_axis=0, concat_axis=0, tiled=True)
    items = lax.all_to_all(
        jnp.concatenate(reduced, axis=1), "dom", split_axis=0, concat_axis=0, tiled=True
    )
    summed = sum_blocks(target.reshape(N_DOM * SLOTS), items)
    pieces = lax.all_to_all(
        summed.reshape(N_DOM, OWN, PIECE, LANES), "dom", split_axis=0, concat_axis=0, tiled=True
    )
    return turn_back(pieces)


def solution(mesh):
    in_specs = (
        P("dom", "grp", None),
        P("dom", None, "grp", None),
        P("dom", None, "grp"),
        P("dom", None, None),
        P("dom", None),
    )
    out_specs = P("dom", "grp", None)
    return jax.shard_map(
        on_device, mesh=mesh, in_specs=in_specs, out_specs=out_specs, check_vma=False
    )
```

```python
import functools
import jax
import jax.numpy as jnp
from jax import lax
from jax.experimental import pallas as pl
from jax.experimental.pallas import tpu as pltpu
from jax.sharding import PartitionSpec as P

BLK = 1024
COLS = 512
SLOTS = 6
OWN = 4
N_DOM = 16
N_GRP = 8
N_Z = 4
LANES = BLK // N_GRP
PIECE = COLS // N_DOM
TAIL = 8
CHUNKS = ((0, 4), (4, 2))
CONTRACT_ROWS = (((0,), (0,)), ((), ()))
VMEM_LIMIT = 24 << 20


def whole_vmem():
    return pl.BlockSpec(memory_space=pltpu.VMEM)


def whole_smem():
    return pl.BlockSpec(memory_space=pltpu.SMEM)


def plane_and_core():
    group = lax.axis_index("grp")
    return lax.div(group, 2), lax.rem(group, 2)


def product_kernel(first, mask, factor, *refs):
    *couplings, own, other = refs
    core = plane_and_core()[1]
    slot = pl.program_id(0)
    present = mask[first + slot].astype(jnp.float32).astype(jnp.bfloat16)
    for k, coupling in enumerate(couplings):
        both = lax.dot_general(
            factor[0], coupling[...], CONTRACT_ROWS, preferred_element_type=jnp.float32
        )
        both = both.astype(jnp.bfloat16) * present
        low, high = both[:, :LANES], both[:, LANES:]
        own[k, :, slot] = jnp.where(core == 0, low, high).reshape(N_DOM, PIECE, LANES)
        other[k, :, slot] = jnp.where(core == 0, high, low).reshape(N_DOM, PIECE, LANES)


def coupling_spec(first, k):
    def block(s):
        return 0, first + s, 0, lax.rem(plane_and_core()[0] + k, N_Z)

    return pl.BlockSpec((None, None, BLK, 2 * LANES), block)


def product(solved, e_blocks, mask, first, count):
    shape = jax.ShapeDtypeStruct((N_Z, N_DOM, count, PIECE, LANES), jnp.bfloat16)
    return pl.pallas_call(
        functools.partial(product_kernel, first),
        grid=(count,),
        in_specs=[whole_smem(), pl.BlockSpec((1, BLK, COLS), lambda s: (0, 0, 0))]
        + [coupling_spec(first, k) for k in range(N_Z)],
        out_specs=[whole_vmem()] * 2,
        out_shape=[shape] * 2,
        compiler_params=pltpu.CompilerParams(vmem_limit_bytes=VMEM_LIMIT),
        name="product",
    )(mask, solved, *[e_blocks] * N_Z)


def finish_kernel(owner, local, *refs):
    *parts, out = refs
    for (first, count), (own, twin, low, high) in zip(CHUNKS, zip(*[iter(parts)] * 4)):
        for s in range(count):
            total = (
                own[0, :, s].astype(jnp.float32)
                + twin[0, :, s].astype(jnp.float32)
                + low[:, s].astype(jnp.float32)
                + high[:, s].astype(jnp.float32)
            )
            rows = slice((first + s) * PIECE, (first + s + 1) * PIECE)
            out[:, rows] = total.astype(jnp.bfloat16)
    lane = lax.broadcasted_iota(jnp.int32, (TAIL, LANES), 1)
    labels = jnp.zeros((TAIL, LANES), jnp.int32)
    for s in range(SLOTS):
        labels = jnp.where(lane == s, owner[s] * OWN + local[s], labels)
    labels = labels.astype(jnp.float32).astype(jnp.bfloat16)
    out[:, SLOTS * PIECE :] = jnp.broadcast_to(labels[None], (N_DOM, TAIL, LANES))


def finish(owner, local_id, parts):
    return pl.pallas_call(
        finish_kernel,
        in_specs=[whole_smem()] * 2 + [whole_vmem()] * len(parts),
        out_specs=whole_vmem(),
        out_shape=jax.ShapeDtypeStruct((N_DOM, SLOTS * PIECE + TAIL, LANES), jnp.bfloat16),
        compiler_params=pltpu.CompilerParams(vmem_limit_bytes=VMEM_LIMIT),
        name="finish",
    )(owner, local_id, *parts)


def sum_kernel(target, items, out, total):
    total[...] = jnp.zeros_like(total)

    def add(i, _):
        for s in range(SLOTS):
            t = target[i * SLOTS + s]
            rows = items[i, s * PIECE : (s + 1) * PIECE]
            total[t] = total[t] + rows.astype(jnp.float32)
        return 0

    lax.fori_loop(0, N_DOM, add, 0)
    out[...] = total[...].astype(jnp.bfloat16)


def sum_blocks(target, items):
    shape = (N_DOM * OWN, PIECE, LANES)
    return pl.pallas_call(
        sum_kernel,
        in_specs=[whole_smem(), whole_vmem()],
        out_specs=whole_vmem(),
        out_shape=jax.ShapeDtypeStruct(shape, jnp.bfloat16),
        scratch_shapes=[pltpu.VMEM(shape, jnp.float32)],
        compiler_params=pltpu.CompilerParams(vmem_limit_bytes=VMEM_LIMIT),
        name="sum_blocks",
    )(target, items)


def turn_kernel(pieces, out):
    for l in range(OWN):
        out[l] = pieces[:, l].reshape(COLS, LANES).T


def turn_back(pieces):
    return pl.pallas_call(
        turn_kernel,
        in_specs=[whole_vmem()],
        out_specs=whole_vmem(),
        out_shape=jax.ShapeDtypeStruct((OWN, LANES, COLS), jnp.bfloat16),
        compiler_params=pltpu.CompilerParams(vmem_limit_bytes=VMEM_LIMIT),
        name="turn_back",
    )(pieces)


def total_of(*terms):
    acc = terms[0].astype(jnp.float32)
    for term in terms[1:]:
        acc = acc + term.astype(jnp.float32)
    return acc.astype(jnp.bfloat16)


def shift_z(k):
    return [(g, ((g // 2 + k) % N_Z) * 2 + g % 2) for g in range(N_GRP)]


def exchange(x):
    return lax.all_to_all(x, "dom", split_axis=0, concat_axis=0, tiled=True)


def on_device(solved, e_blocks, block_mask, owner, local_id):
    solved = pltpu.with_memory_space_constraint(solved, pltpu.HBM)
    e_blocks = pltpu.with_memory_space_constraint(e_blocks, pltpu.HBM)
    mask = pltpu.with_memory_space_constraint(block_mask.reshape(SLOTS), pltpu.HBM)
    sibling = [(g, g ^ 1) for g in range(N_GRP)]
    half = N_DOM // 2
    parts = []
    for first, count in CHUNKS:
        own, other = product(solved, e_blocks, mask, first, count)
        twin = lax.ppermute(other, "grp", sibling)
        far_up = total_of(own[2, :half], twin[2, :half])
        far_down = total_of(own[2, half:], twin[2, half:])
        from_below = lax.ppermute(far_up, "grp", shift_z(1))
        from_above = lax.ppermute(far_down, "grp", shift_z(-1))
        up = jnp.concatenate(
            [total_of(own[1, :half], twin[1, :half], from_below), total_of(own[1, half:], twin[1, half:])]
        )
        down = jnp.concatenate(
            [total_of(own[3, :half], twin[3, :half]), total_of(own[3, half:], twin[3, half:], from_above)]
        )
        low = lax.ppermute(up, "grp", shift_z(1))
        high = lax.ppermute(down, "grp", shift_z(-1))
        parts += [own, twin, low, high]
    items = exchange(finish(owner.reshape(SLOTS), local_id.reshape(SLOTS), parts))
    target = items[:, SLOTS * PIECE, :SLOTS].astype(jnp.int32)
    summed = sum_blocks(target.reshape(N_DOM * SLOTS), items)
    pieces = exchange(summed.reshape(N_DOM, OWN, PIECE, LANES))
    return turn_back(pieces)


def solution(mesh):
    in_specs = (
        P("dom", "grp", None),
        P("dom", None, "grp", None),
        P("dom", None, "grp"),
        P("dom", None, None),
        P("dom", None),
    )
    out_specs = P("dom", "grp", None)
    return jax.shard_map(
        on_device, mesh=mesh, in_specs=in_specs, out_specs=out_specs, check_vma=False
    )
```

```python
import functools
import jax
import jax.numpy as jnp
from jax import lax
from jax.experimental import pallas as pl
from jax.experimental.pallas import tpu as pltpu
from jax.sharding import PartitionSpec as P

BLK = 1024
COLS = 512
SLOTS = 6
OWN = 4
N_DOM = 16
N_GRP = 8
N_Z = 4
LANES = BLK // N_GRP
PIECE = COLS // N_DOM
TAIL = 8
CHUNKS = ((0, 4), (4, 2))
CONTRACT_ROWS = (((0,), (0,)), ((), ()))
VMEM_LIMIT = 24 << 20


def whole_vmem():
    return pl.BlockSpec(memory_space=pltpu.VMEM)


def whole_smem():
    return pl.BlockSpec(memory_space=pltpu.SMEM)


def plane_and_core():
    group = lax.axis_index("grp")
    return lax.div(group, 2), lax.rem(group, 2)


def product_kernel(first, mask, factor, *refs):
    *couplings, own, other = refs
    core = plane_and_core()[1]
    slot = pl.program_id(0)
    present = mask[first + slot].astype(jnp.float32).astype(jnp.bfloat16)
    for k, coupling in enumerate(couplings):
        both = lax.dot_general(
            factor[0], coupling[...], CONTRACT_ROWS, preferred_element_type=jnp.float32
        )
        both = both.astype(jnp.bfloat16) * present
        low, high = both[:, :LANES], both[:, LANES:]
        own[k, :, slot] = jnp.where(core == 0, low, high).reshape(N_DOM, PIECE, LANES)
        other[k, :, slot] = jnp.where(core == 0, high, low).reshape(N_DOM, PIECE, LANES)


def coupling_spec(first, k):
    def block(s):
        return 0, first + s, 0, lax.rem(plane_and_core()[0] + k, N_Z)

    return pl.BlockSpec((None, None, BLK, 2 * LANES), block)


def product(solved, e_blocks, mask, first, count):
    shape = jax.ShapeDtypeStruct((N_Z, N_DOM, count, PIECE, LANES), jnp.bfloat16)
    return pl.pallas_call(
        functools.partial(product_kernel, first),
        grid=(count,),
        in_specs=[whole_smem(), pl.BlockSpec((1, BLK, COLS), lambda s: (0, 0, 0))]
        + [coupling_spec(first, k) for k in range(N_Z)],
        out_specs=[whole_vmem()] * 2,
        out_shape=[shape] * 2,
        compiler_params=pltpu.CompilerParams(vmem_limit_bytes=VMEM_LIMIT),
        name="product",
    )(mask, solved, *[e_blocks] * N_Z)


def finish_kernel(first, count, *refs):
    *labels, own, twin, low, high = refs[:-1] if first == 0 else refs[1:-1]
    out = refs[-1]
    for s in range(count):
        total = (
            own[0, :, s].astype(jnp.float32)
            + twin[0, :, s].astype(jnp.float32)
            + low[:, s].astype(jnp.float32)
            + high[:, s].astype(jnp.float32)
        )
        rows = slice((first + s) * PIECE, (first + s + 1) * PIECE)
        out[:, rows] = total.astype(jnp.bfloat16)
    if labels:
        owner, local = labels
        lane = lax.broadcasted_iota(jnp.int32, (TAIL, LANES), 1)
        tail = jnp.zeros((TAIL, LANES), jnp.int32)
        for s in range(SLOTS):
            tail = jnp.where(lane == s, owner[s] * OWN + local[s], tail)
        tail = tail.astype(jnp.float32).astype(jnp.bfloat16)
        out[:, SLOTS * PIECE :] = jnp.broadcast_to(tail[None], (N_DOM, TAIL, LANES))


def finish(first, count, head, *parts):
    return pl.pallas_call(
        functools.partial(finish_kernel, first, count),
        in_specs=([whole_vmem()] if first else [whole_smem()] * 2) + [whole_vmem()] * len(parts),
        out_specs=whole_vmem(),
        out_shape=jax.ShapeDtypeStruct((N_DOM, SLOTS * PIECE + TAIL, LANES), jnp.bfloat16),
        input_output_aliases={0: 0} if first else {},
        compiler_params=pltpu.CompilerParams(vmem_limit_bytes=VMEM_LIMIT),
        name="finish",
    )(*head, *parts)


def sum_kernel(target, items, out, total):
    total[...] = jnp.zeros_like(total)

    def add(i, _):
        for s in range(SLOTS):
            t = target[i * SLOTS + s]
            rows = items[i, s * PIECE : (s + 1) * PIECE]
            total[t] = total[t] + rows.astype(jnp.float32)
        return 0

    lax.fori_loop(0, N_DOM, add, 0)
    out[...] = total[...].astype(jnp.bfloat16)


def sum_blocks(target, items):
    shape = (N_DOM * OWN, PIECE, LANES)
    return pl.pallas_call(
        sum_kernel,
        in_specs=[whole_smem(), whole_vmem()],
        out_specs=whole_vmem(),
        out_shape=jax.ShapeDtypeStruct(shape, jnp.bfloat16),
        scratch_shapes=[pltpu.VMEM(shape, jnp.float32)],
        compiler_params=pltpu.CompilerParams(vmem_limit_bytes=VMEM_LIMIT),
        name="sum_blocks",
    )(target, items)


def turn_kernel(pieces, out):
    for l in range(OWN):
        out[l] = pieces[:, l].reshape(COLS, LANES).T


def turn_back(pieces):
    return pl.pallas_call(
        turn_kernel,
        in_specs=[whole_vmem()],
        out_specs=whole_vmem(),
        out_shape=jax.ShapeDtypeStruct((OWN, LANES, COLS), jnp.bfloat16),
        compiler_params=pltpu.CompilerParams(vmem_limit_bytes=VMEM_LIMIT),
        name="turn_back",
    )(pieces)


def total_of(*terms):
    acc = terms[0].astype(jnp.float32)
    for term in terms[1:]:
        acc = acc + term.astype(jnp.float32)
    return acc.astype(jnp.bfloat16)


def shift_z(k):
    return [(g, ((g // 2 + k) % N_Z) * 2 + g % 2) for g in range(N_GRP)]


def exchange(x):
    return lax.all_to_all(x, "dom", split_axis=0, concat_axis=0, tiled=True)


def on_device(solved, e_blocks, block_mask, owner, local_id):
    pinned = pltpu.with_memory_space_constraint(solved, pltpu.HBM)
    e_blocks = pltpu.with_memory_space_constraint(e_blocks, pltpu.HBM)
    mask = pltpu.with_memory_space_constraint(block_mask.reshape(SLOTS), pltpu.HBM)
    sibling = [(g, g ^ 1) for g in range(N_GRP)]
    half = N_DOM // 2
    outgoing = None
    for first, count in CHUNKS:
        own, other = product(solved if first else pinned, e_blocks, mask, first, count)
        twin = lax.ppermute(other, "grp", sibling)
        far_up = total_of(own[2, :half], twin[2, :half])
        far_down = total_of(own[2, half:], twin[2, half:])
        from_below = lax.ppermute(far_up, "grp", shift_z(1))
        from_above = lax.ppermute(far_down, "grp", shift_z(-1))
        up = jnp.concatenate(
            [total_of(own[1, :half], twin[1, :half], from_below), total_of(own[1, half:], twin[1, half:])]
        )
        down = jnp.concatenate(
            [total_of(own[3, :half], twin[3, :half]), total_of(own[3, half:], twin[3, half:], from_above)]
        )
        low = lax.ppermute(up, "grp", shift_z(1))
        high = lax.ppermute(down, "grp", shift_z(-1))
        head = (outgoing,) if first else (owner.reshape(SLOTS), local_id.reshape(SLOTS))
        outgoing = finish(first, count, head, own, twin, low, high)
    items = exchange(outgoing)
    target = items[:, SLOTS * PIECE, :SLOTS].astype(jnp.int32)
    summed = sum_blocks(target.reshape(N_DOM * SLOTS), items)
    pieces = exchange(summed.reshape(N_DOM, OWN, PIECE, LANES))
    return turn_back(pieces)


def solution(mesh):
    in_specs = (
        P("dom", "grp", None),
        P("dom", None, "grp", None),
        P("dom", None, "grp"),
        P("dom", None, None),
        P("dom", None),
    )
    out_specs = P("dom", "grp", None)
    return jax.shard_map(
        on_device, mesh=mesh, in_specs=in_specs, out_specs=out_specs, check_vma=False
    )
```

```python
import functools
import jax
import jax.numpy as jnp
from jax import lax
from jax.experimental import pallas as pl
from jax.experimental.pallas import tpu as pltpu
from jax.sharding import PartitionSpec as P

BLK = 1024
COLS = 512
SLOTS = 6
OWN = 4
N_DOM = 16
N_GRP = 8
N_Z = 4
LANES = BLK // N_GRP
PIECE = COLS // N_DOM
TAIL = 8
CHUNKS = ((0, 3), (3, 3))
CONTRACT_ROWS = (((0,), (0,)), ((), ()))
VMEM_LIMIT = 24 << 20


def whole_vmem():
    return pl.BlockSpec(memory_space=pltpu.VMEM)


def whole_smem():
    return pl.BlockSpec(memory_space=pltpu.SMEM)


def plane_and_core():
    group = lax.axis_index("grp")
    return lax.div(group, 2), lax.rem(group, 2)


def product_kernel(first, mask, factor, *refs):
    *couplings, own, other = refs
    core = plane_and_core()[1]
    slot = pl.program_id(0)
    present = mask[first + slot].astype(jnp.float32).astype(jnp.bfloat16)
    for k, coupling in enumerate(couplings):
        both = lax.dot_general(
            factor[0], coupling[...], CONTRACT_ROWS, preferred_element_type=jnp.float32
        )
        both = both.astype(jnp.bfloat16) * present
        low, high = both[:, :LANES], both[:, LANES:]
        own[k, :, slot] = jnp.where(core == 0, low, high).reshape(N_DOM, PIECE, LANES)
        other[k, :, slot] = jnp.where(core == 0, high, low).reshape(N_DOM, PIECE, LANES)


def coupling_spec(first, k):
    def block(s):
        return 0, first + s, 0, lax.rem(plane_and_core()[0] + k, N_Z)

    return pl.BlockSpec((None, None, BLK, 2 * LANES), block)


def product(solved, e_blocks, mask, first, count):
    shape = jax.ShapeDtypeStruct((N_Z, N_DOM, count, PIECE, LANES), jnp.bfloat16)
    return pl.pallas_call(
        functools.partial(product_kernel, first),
        grid=(count,),
        in_specs=[whole_smem(), pl.BlockSpec((1, BLK, COLS), lambda s: (0, 0, 0))]
        + [coupling_spec(first, k) for k in range(N_Z)],
        out_specs=[whole_vmem()] * 2,
        out_shape=[shape] * 2,
        compiler_params=pltpu.CompilerParams(vmem_limit_bytes=VMEM_LIMIT),
        name="product",
    )(mask, solved, *[e_blocks] * N_Z)


def finish_kernel(first, count, *refs):
    *labels, own, twin, below, above, low, high = refs[:-1] if first == 0 else refs[1:-1]
    out = refs[-1]
    half = N_DOM // 2
    for s in range(count):
        rows = slice((first + s) * PIECE, (first + s + 1) * PIECE)
        for here, ring in (
            (slice(0, half), (above[half:, s], low[:, s])),
            (slice(half, N_DOM), (below[:half, s], high[:, s])),
        ):
            total = own[0, here, s].astype(jnp.float32) + twin[0, here, s].astype(jnp.float32)
            for term in ring:
                total = total + term.astype(jnp.float32)
            out[here, rows] = total.astype(jnp.bfloat16)
    if labels:
        owner, local = labels
        lane = lax.broadcasted_iota(jnp.int32, (TAIL, LANES), 1)
        tail = jnp.zeros((TAIL, LANES), jnp.int32)
        for s in range(SLOTS):
            tail = jnp.where(lane == s, owner[s] * OWN + local[s], tail)
        tail = tail.astype(jnp.float32).astype(jnp.bfloat16)
        out[:, SLOTS * PIECE :] = jnp.broadcast_to(tail[None], (N_DOM, TAIL, LANES))


def finish(first, count, head, *parts):
    return pl.pallas_call(
        functools.partial(finish_kernel, first, count),
        in_specs=([whole_vmem()] if first else [whole_smem()] * 2) + [whole_vmem()] * len(parts),
        out_specs=whole_vmem(),
        out_shape=jax.ShapeDtypeStruct((N_DOM, SLOTS * PIECE + TAIL, LANES), jnp.bfloat16),
        input_output_aliases={0: 0} if first else {},
        compiler_params=pltpu.CompilerParams(vmem_limit_bytes=VMEM_LIMIT),
        name="finish",
    )(*head, *parts)


def sum_kernel(target, items, out, total):
    total[...] = jnp.zeros_like(total)

    def add(i, _):
        for s in range(SLOTS):
            t = target[i * SLOTS + s]
            rows = items[i, s * PIECE : (s + 1) * PIECE]
            total[t] = total[t] + rows.astype(jnp.float32)
        return 0

    lax.fori_loop(0, N_DOM, add, 0)
    out[...] = total[...].astype(jnp.bfloat16)


def sum_blocks(target, items):
    shape = (N_DOM * OWN, PIECE, LANES)
    return pl.pallas_call(
        sum_kernel,
        in_specs=[whole_smem(), whole_vmem()],
        out_specs=whole_vmem(),
        out_shape=jax.ShapeDtypeStruct(shape, jnp.bfloat16),
        scratch_shapes=[pltpu.VMEM(shape, jnp.float32)],
        compiler_params=pltpu.CompilerParams(vmem_limit_bytes=VMEM_LIMIT),
        name="sum_blocks",
    )(target, items)


def turn_kernel(pieces, out):
    for l in range(OWN):
        out[l] = pieces[:, l].reshape(COLS, LANES).T


def turn_back(pieces):
    return pl.pallas_call(
        turn_kernel,
        in_specs=[whole_vmem()],
        out_specs=whole_vmem(),
        out_shape=jax.ShapeDtypeStruct((OWN, LANES, COLS), jnp.bfloat16),
        compiler_params=pltpu.CompilerParams(vmem_limit_bytes=VMEM_LIMIT),
        name="turn_back",
    )(pieces)


def total_of(*terms):
    acc = terms[0].astype(jnp.float32)
    for term in terms[1:]:
        acc = acc + term.astype(jnp.float32)
    return acc.astype(jnp.bfloat16)


def shift_z(k):
    return [(g, ((g // 2 + k) % N_Z) * 2 + g % 2) for g in range(N_GRP)]


def exchange(x):
    return lax.all_to_all(x, "dom", split_axis=0, concat_axis=0, tiled=True)


def on_device(solved, e_blocks, block_mask, owner, local_id):
    pinned = pltpu.with_memory_space_constraint(solved, pltpu.HBM)
    e_blocks = pltpu.with_memory_space_constraint(e_blocks, pltpu.HBM)
    mask = pltpu.with_memory_space_constraint(block_mask.reshape(SLOTS), pltpu.HBM)
    sibling = [(g, g ^ 1) for g in range(N_GRP)]
    half = N_DOM // 2
    outgoing = None
    for first, count in CHUNKS:
        own, other = product(solved if first else pinned, e_blocks, mask, first, count)
        twin = lax.ppermute(other, "grp", sibling)
        flat = (N_Z * N_DOM, count, PIECE, LANES)
        mine, yours = own.reshape(flat), twin.reshape(flat)

        def both(start, stop, *more):
            return total_of(mine[start:stop], yours[start:stop], *more)

        below = lax.ppermute(both(3 * half, 5 * half), "grp", shift_z(1))
        above = lax.ppermute(both(5 * half, 7 * half), "grp", shift_z(-1))
        low = lax.ppermute(both(2 * half, 3 * half, below[half:]), "grp", shift_z(1))
        high = lax.ppermute(both(7 * half, 8 * half, above[:half]), "grp", shift_z(-1))
        head = (outgoing,) if first else (owner.reshape(SLOTS), local_id.reshape(SLOTS))
        outgoing = finish(first, count, head, own, twin, below, above, low, high)
    items = exchange(outgoing)
    target = items[:, SLOTS * PIECE, :SLOTS].astype(jnp.int32)
    summed = sum_blocks(target.reshape(N_DOM * SLOTS), items)
    pieces = exchange(summed.reshape(N_DOM, OWN, PIECE, LANES))
    return turn_back(pieces)


def solution(mesh):
    in_specs = (
        P("dom", "grp", None),
        P("dom", None, "grp", None),
        P("dom", None, "grp"),
        P("dom", None, None),
        P("dom", None),
    )
    out_specs = P("dom", "grp", None)
    return jax.shard_map(
        on_device, mesh=mesh, in_specs=in_specs, out_specs=out_specs, check_vma=False
    )
```

```python
import functools
import jax
import jax.numpy as jnp
from jax import lax
from jax.experimental import pallas as pl
from jax.experimental.pallas import tpu as pltpu
from jax.sharding import PartitionSpec as P

BLK = 1024
COLS = 512
SLOTS = 6
OWN = 4
N_DOM = 16
N_GRP = 8
N_Z = 4
LANES = BLK // N_GRP
PIECE = COLS // N_DOM
TAIL = 8
CHUNKS = ((0, 3), (3, 3))
CONTRACT_ROWS = (((0,), (0,)), ((), ()))
VMEM_LIMIT = 24 << 20


def whole_vmem():
    return pl.BlockSpec(memory_space=pltpu.VMEM)


def whole_smem():
    return pl.BlockSpec(memory_space=pltpu.SMEM)


def plane_and_core():
    group = lax.axis_index("grp")
    return lax.div(group, 2), lax.rem(group, 2)


def product_kernel(first, mask, factor, *refs):
    *couplings, own, other = refs
    core = plane_and_core()[1]
    slot = pl.program_id(0)
    present = mask[first + slot].astype(jnp.float32).astype(jnp.bfloat16)
    for k, coupling in enumerate(couplings):
        both = lax.dot_general(
            factor[0], coupling[...], CONTRACT_ROWS, preferred_element_type=jnp.float32
        )
        both = both.astype(jnp.bfloat16) * present
        low, high = both[:, :LANES], both[:, LANES:]
        own[k, :, slot] = jnp.where(core == 0, low, high).reshape(N_DOM, PIECE, LANES)
        other[k, :, slot] = jnp.where(core == 0, high, low).reshape(N_DOM, PIECE, LANES)


def coupling_spec(first, k):
    def block(s):
        return 0, first + s, 0, lax.rem(plane_and_core()[0] + k, N_Z)

    return pl.BlockSpec((None, None, BLK, 2 * LANES), block)


def product(solved, e_blocks, mask, first, count):
    shape = jax.ShapeDtypeStruct((N_Z, N_DOM, count, PIECE, LANES), jnp.bfloat16)
    return pl.pallas_call(
        functools.partial(product_kernel, first),
        grid=(count,),
        in_specs=[whole_smem(), pl.BlockSpec((1, BLK, COLS), lambda s: (0, 0, 0))]
        + [coupling_spec(first, k) for k in range(N_Z)],
        out_specs=[whole_vmem()] * 2,
        out_shape=[shape] * 2,
        compiler_params=pltpu.CompilerParams(vmem_limit_bytes=VMEM_LIMIT),
        name="product",
    )(mask, solved, *[e_blocks] * N_Z)


def finish_kernel(first, count, *refs):
    *labels, own, twin, below, above, low, high = refs[:-1] if first == 0 else refs[1:-1]
    out = refs[-1]
    half = N_DOM // 2
    for s in range(count):
        rows = slice((first + s) * PIECE, (first + s + 1) * PIECE)
        for here, ring in (
            (slice(0, half), (above[half:, s], low[:, s])),
            (slice(half, N_DOM), (below[:half, s], high[:, s])),
        ):
            total = own[0, here, s].astype(jnp.float32) + twin[0, here, s].astype(jnp.float32)
            for term in ring:
                total = total + term.astype(jnp.float32)
            out[here, rows] = total.astype(jnp.bfloat16)
    if labels:
        owner, local = labels
        lane = lax.broadcasted_iota(jnp.int32, (TAIL, LANES), 1)
        tail = jnp.zeros((TAIL, LANES), jnp.int32)
        for s in range(SLOTS):
            tail = jnp.where(lane == s, owner[s] * OWN + local[s], tail)
        tail = tail.astype(jnp.float32).astype(jnp.bfloat16)
        out[:, SLOTS * PIECE :] = jnp.broadcast_to(tail[None], (N_DOM, TAIL, LANES))


def finish(first, count, head, *parts):
    return pl.pallas_call(
        functools.partial(finish_kernel, first, count),
        in_specs=([whole_vmem()] if first else [whole_smem()] * 2) + [whole_vmem()] * len(parts),
        out_specs=whole_vmem(),
        out_shape=jax.ShapeDtypeStruct((N_DOM, SLOTS * PIECE + TAIL, LANES), jnp.bfloat16),
        input_output_aliases={0: 0} if first else {},
        compiler_params=pltpu.CompilerParams(vmem_limit_bytes=VMEM_LIMIT),
        name="finish",
    )(*head, *parts)


def sum_kernel(target, items, out, total):
    total[...] = jnp.zeros_like(total)

    def add(i, _):
        for s in range(SLOTS):
            t = target[i * SLOTS + s]
            rows = items[i, s * PIECE : (s + 1) * PIECE]
            total[t] = total[t] + rows.astype(jnp.float32)
        return 0

    lax.fori_loop(0, N_DOM, add, 0)
    out[...] = total[...].astype(jnp.bfloat16)


def sum_blocks(target, items):
    shape = (N_DOM * OWN, PIECE, LANES)
    return pl.pallas_call(
        sum_kernel,
        in_specs=[whole_smem(), whole_vmem()],
        out_specs=whole_vmem(),
        out_shape=jax.ShapeDtypeStruct(shape, jnp.bfloat16),
        scratch_shapes=[pltpu.VMEM(shape, jnp.float32)],
        compiler_params=pltpu.CompilerParams(vmem_limit_bytes=VMEM_LIMIT),
        name="sum_blocks",
    )(target, items)


def turn_kernel(pieces, out, turned, sems):
    copies = []
    for l in range(OWN):
        turned[l] = pieces[:, l].reshape(COLS, LANES).T
        copies.append(pltpu.make_async_copy(turned.at[l], out.at[l], sems.at[l]))
        copies[l].start()
    for copy in copies:
        copy.wait()


def turn_back(pieces):
    shape = (OWN, LANES, COLS)
    return pl.pallas_call(
        turn_kernel,
        in_specs=[whole_vmem()],
        out_specs=pl.BlockSpec(memory_space=pl.ANY),
        out_shape=jax.ShapeDtypeStruct(shape, jnp.bfloat16),
        scratch_shapes=[pltpu.VMEM(shape, jnp.bfloat16), pltpu.SemaphoreType.DMA((OWN,))],
        compiler_params=pltpu.CompilerParams(vmem_limit_bytes=VMEM_LIMIT),
        name="turn_back",
    )(pieces)


def total_of(*terms):
    acc = terms[0].astype(jnp.float32)
    for term in terms[1:]:
        acc = acc + term.astype(jnp.float32)
    return acc.astype(jnp.bfloat16)


def shift_z(k):
    return [(g, ((g // 2 + k) % N_Z) * 2 + g % 2) for g in range(N_GRP)]


def exchange(x):
    return lax.all_to_all(x, "dom", split_axis=0, concat_axis=0, tiled=True)


def on_device(solved, e_blocks, block_mask, owner, local_id):
    pinned = pltpu.with_memory_space_constraint(solved, pltpu.HBM)
    e_blocks = pltpu.with_memory_space_constraint(e_blocks, pltpu.HBM)
    mask = pltpu.with_memory_space_constraint(block_mask.reshape(SLOTS), pltpu.HBM)
    sibling = [(g, g ^ 1) for g in range(N_GRP)]
    half = N_DOM // 2
    outgoing = None
    for first, count in CHUNKS:
        own, other = product(solved if first else pinned, e_blocks, mask, first, count)
        twin = lax.ppermute(other, "grp", sibling)
        flat = (N_Z * N_DOM, count, PIECE, LANES)
        mine, yours = own.reshape(flat), twin.reshape(flat)

        def both(start, stop, *more):
            return total_of(mine[start:stop], yours[start:stop], *more)

        below = lax.ppermute(both(3 * half, 5 * half), "grp", shift_z(1))
        above = lax.ppermute(both(5 * half, 7 * half), "grp", shift_z(-1))
        low = lax.ppermute(both(2 * half, 3 * half, below[half:]), "grp", shift_z(1))
        high = lax.ppermute(both(7 * half, 8 * half, above[:half]), "grp", shift_z(-1))
        head = (outgoing,) if first else (owner.reshape(SLOTS), local_id.reshape(SLOTS))
        outgoing = finish(first, count, head, own, twin, below, above, low, high)
    items = exchange(outgoing)
    target = items[:, SLOTS * PIECE, :SLOTS].astype(jnp.int32)
    summed = sum_blocks(target.reshape(N_DOM * SLOTS), items)
    pieces = exchange(summed.reshape(N_DOM, OWN, PIECE, LANES))
    return turn_back(pieces)


def solution(mesh):
    in_specs = (
        P("dom", "grp", None),
        P("dom", None, "grp", None),
        P("dom", None, "grp"),
        P("dom", None, None),
        P("dom", None),
    )
    out_specs = P("dom", "grp", None)
    return jax.shard_map(
        on_device, mesh=mesh, in_specs=in_specs, out_specs=out_specs, check_vma=False
    )
```
